256 devices in a mesh: chain: 128 (over y_hi, x, z, core), col: 2 (over y_lo).
Axes of the slice: x: 4, y: 4 (y_hi: 2, y_lo: 2; y = y_hi * 2 + y_lo), z: 8, core: 2. Of those that a mesh axis runs over, the one named last changes fastest.
Arguments:
- diag_inverse: float32 [2048, 128, 128], P(('chain', 'col'))
- off_blocks: float32 [4096, 128, 128], P(('chain', 'col')), may hold values from -0.1875 to 0.1875
- off_row: int32 [4096], P(('chain', 'col')), may hold values from 0 to 15, as said below
- off_col: int32 [4096], P(('chain', 'col')), may hold values from 0 to 15, as said below
- rhs: float32 [5, 262144, 256], P(None, ('chain', 'col')), may hold values from -8 to 8
- front_in: float32 [262144, 256], P(('chain', 'col')), may hold values from -4 to 4
Outputs:
- solutions: float32 [5, 262144, 256], P(None, ('chain', 'col'))
- front_out: float32 [262144, 256], P(('chain', 'col'))
The draws below stay inside these ranges and needn't reach their ends.
Inputs may be any that keep to these rules, and one draw needn't show every extreme that they name: `off_col`: the blocks of a section are laid out in 2 runs of 16; the blocks of run k name column supernodes k * 8 to (k + 1) * 8 - 1 only, and no two blocks of a section name the same pair of row and column supernodes. `off_row`: no two blocks of a section name the same pair of row and column supernodes.
All inputs are finite; a program needn't handle non-finite values.
Results may differ from the reference program's by a relative error of at most 0.0003.
Values sent between devices are 32-bit elements; how exact they have to be, the bound alone decides.
No kernel may reach another device: no remote copies, remote signals or barrier semaphores. Data moves between devices by JAX's collectives and lax.ppermute only.
A program may use at most 128 MiB of HBM per device.

```python
import jax
import jax.numpy as jnp
from jax import lax

BLOCK = 128
WIDTH = 256
SUP_DEV = 8
NOFF_DEV = 16
TICKS = 5
NB = 16
NOFF = 32
NSUP = 2048
NROWS = 262144
NBLK = 4096


def draw_diag_inverse(key, part):
    first_key, second_key = jax.random.split(jax.random.fold_in(key, 11), 2)
    diagonal = jnp.exp(jax.random.uniform(first_key, (NSUP, BLOCK), jnp.float32, jnp.log(0.5), jnp.log(2.0)))
    noise = jax.random.normal(second_key, (NSUP, BLOCK, BLOCK), jnp.float32) * (0.3 / BLOCK ** 0.5)
    identity = jnp.eye(BLOCK, dtype=jnp.float32)
    return noise + diagonal[:, :, None] * identity[None, :, :]


def pair_codes(key):
    runs = NBLK // NOFF_DEV
    pair_count = NB * SUP_DEV
    base_key = jax.random.fold_in(key, 37)
    run_keys = jax.vmap(lambda index: jax.random.fold_in(base_key, index))(jnp.arange(runs, dtype=jnp.int32))
    orders = jax.vmap(lambda one_key: jax.random.permutation(one_key, pair_count))(run_keys)
    return orders[:, :NOFF_DEV].reshape(NBLK).astype(jnp.int32)


def draw_off_row(key, part):
    codes = pair_codes(key)
    return (codes // SUP_DEV).astype(jnp.int32)


def draw_off_col(key, part):
    codes = pair_codes(key)
    position = jnp.arange(NBLK, dtype=jnp.int32)
    owner = position % NOFF // NOFF_DEV
    return (owner * SUP_DEV + codes % SUP_DEV).astype(jnp.int32)


def levels(stream_key, extent, pieces, least, high):
    def one(dim, shards_of):
        draws = jax.random.uniform(jax.random.fold_in(jax.random.fold_in(stream_key, 6), dim), (shards_of,), jnp.float32, least / len(pieces), high / len(pieces))
        return jnp.repeat(jnp.exp(draws), extent[dim] // shards_of).reshape((-1,) + (1,) * (len(extent) - dim - 1))

    factor_of = one(*pieces[0])
    for cut in pieces[1:]:
        factor_of = factor_of * one(*cut)
    return factor_of


def bell_draw(own_key, shape, spread, most, shards=(), kind=jnp.bfloat16):
    values = jax.random.normal(own_key, shape, jnp.float32) * spread
    if len(shards) > 0:
        values = levels(own_key, shape, shards, -0.22, 0.18) * values
    return jnp.clip(values, min=-most, max=most).astype(kind)


def setup_inputs(seed: int = 0) -> dict:
    splits = jax.random.split(jax.random.key(seed), 7)
    return {
        "diag_inverse": draw_diag_inverse(jax.random.fold_in(splits[6], 71), 0),
        "off_blocks": bell_draw(splits[1], (NBLK, BLOCK, BLOCK), (4 * BLOCK * NOFF // NB) ** -0.5, 0.1875, ((0, 256),), jnp.float32),
        "off_row": draw_off_row(jax.random.fold_in(splits[6], 71), 0),
        "off_col": draw_off_col(jax.random.fold_in(splits[6], 71), 0),
        "rhs": bell_draw(splits[4], (TICKS, NROWS, WIDTH), 1.0, 8.0, ((1, 256),), jnp.float32),
        "front_in": bell_draw(splits[5], (NROWS, WIDTH), 0.5, 4.0, ((0, 256),), jnp.float32),
    }


HIGH = lax.Precision.HIGHEST


def reference(diag_inverse, off_blocks, off_row, off_col, rhs, front_in):
    sections = NSUP // NB
    blocks = off_blocks.reshape(sections, NOFF, BLOCK, BLOCK)
    rows_all = off_row.reshape(sections, NOFF)
    cols_all = off_col.reshape(sections, NOFF)
    front = front_in
    solved_list = []
    for tick_index in range(TICKS):
        shaped = (rhs[tick_index] - front).reshape(NSUP, BLOCK, WIDTH)
        solved = jnp.einsum("nij,njw->niw", diag_inverse, shaped, precision=HIGH)
        solved_list.append(solved.reshape(NROWS, WIDTH))
        by_section = solved.reshape(sections, NB, BLOCK, WIDTH)

        def one_section(items):
            sec_blocks, sec_rows, sec_cols, sec_solved = items
            pick_table = (sec_cols[:, None] == jnp.arange(NB, dtype=jnp.int32)[None, :]).astype(jnp.float32)
            picked = jnp.einsum("kn,niw->kiw", pick_table, sec_solved, precision=HIGH)
            product = jnp.einsum("kij,kjw->kiw", sec_blocks, picked, precision=HIGH)
            row_table = (sec_rows[None, :] == jnp.arange(NB, dtype=jnp.int32)[:, None]).astype(jnp.float32)
            return jnp.einsum("bk,kiw->biw", row_table, product, precision=HIGH)

        partial_value = lax.map(one_section, (blocks, rows_all, cols_all, by_section))
        partial_value = partial_value.reshape(sections, NB * BLOCK, WIDTH)
        zeros_first = jnp.zeros((1, NB * BLOCK, WIDTH), jnp.float32)
        front = jnp.concatenate([zeros_first, partial_value[:-1]], axis=0).reshape(NROWS, WIDTH)
    return jnp.stack(solved_list), front
```

```python
import jax
import jax.numpy as jnp
from jax import lax
from jax.sharding import PartitionSpec as P

HIGH = lax.Precision.HIGH
CHUNKS = 2


def shifted(value, axis, steps):
    count = lax.axis_size(axis)
    initial, last = (max(0, -steps), min(count, count - steps))
    return lax.ppermute(value, axis, [(source, source + steps) for source in range(initial, last)])


def local(diag_inverse, off_blocks, off_row, off_col, rhs, front_in):
    sup_local, block_size, _ = diag_inverse.shape
    tick_count, rows, width_cols = rhs.shape
    halves = lax.axis_size("col")
    sup_section = sup_local * halves
    col_start = lax.axis_index("col") * sup_local
    pick_table = (
        off_col[:, None] - col_start == jnp.arange(sup_local, dtype=jnp.int32)[None, :]
    ).astype(jnp.float32)
    row_local = (off_row - col_start) % sup_section
    row_table = (row_local[:, None] == jnp.arange(sup_section, dtype=jnp.int32)[None, :]).astype(
        jnp.float32
    )
    pair_table = row_table[:, :, None] * pick_table[:, None, :]
    coupling = jnp.einsum("kbn,kij->binj", pair_table, off_blocks, precision=HIGH)
    coupling = coupling.reshape(sup_section * block_size, sup_local * block_size)
    mine, other = coupling[:rows], coupling[rows:]
    width = width_cols // CHUNKS
    fronts = [front_in[:, c * width : (c + 1) * width] for c in range(CHUNKS)]
    solved_rows = []
    for tick_index in range(tick_count):
        solved_chunks = []
        for c in range(CHUNKS):
            values = rhs[tick_index, :, c * width : (c + 1) * width] - fronts[c]
            shaped = values.reshape(sup_local, block_size, width)
            solved = jnp.einsum("nij,njw->niw", diag_inverse, shaped, precision=HIGH)
            flat = solved.reshape(rows, width)
            solved_chunks.append(flat)
            send = jnp.dot(other, flat, precision=HIGH)
            arrived = lax.ppermute(send, "col", [(i, halves - 1 - i) for i in range(halves)])
            kept = jnp.dot(mine, flat, precision=HIGH)
            fronts[c] = shifted(kept + arrived, "chain", 1)
        solved_rows.append(jnp.concatenate(solved_chunks, axis=1))
    return (jnp.stack(solved_rows), jnp.concatenate(fronts, axis=1))


def solution(mesh):
    return jax.shard_map(
        local,
        mesh=mesh,
        in_specs=(
            P(("chain", "col"), None, None),
            P(("chain", "col"), None, None),
            P(("chain", "col")),
            P(("chain", "col")),
            P(None, ("chain", "col"), None),
            P(("chain", "col"), None),
        ),
        out_specs=(P(None, ("chain", "col"), None), P(("chain", "col"), None)),
        check_vma=False,
    )
```

```python
import jax
import jax.numpy as jnp
from jax import lax
from jax.sharding import PartitionSpec as P

HIGH = lax.Precision.HIGH
CHUNKS = 2


def local(diag_inverse, off_blocks, off_row, off_col, rhs, front_in):
    sup_local, block_size, _ = diag_inverse.shape
    tick_count, rows, width_cols = rhs.shape
    halves = lax.axis_size("col")
    sup_section = sup_local * halves
    col_start = lax.axis_index("col") * sup_local
    pick_table = (
        off_col[:, None] - col_start == jnp.arange(sup_local, dtype=jnp.int32)[None, :]
    ).astype(jnp.float32)
    row_local = (off_row - col_start) % sup_section
    row_table = (row_local[:, None] == jnp.arange(sup_section, dtype=jnp.int32)[None, :]).astype(
        jnp.float32
    )
    pair_table = row_table[:, :, None] * pick_table[:, None, :]
    coupling = jnp.einsum("kbn,kij->binj", pair_table, off_blocks, precision=HIGH)
    coupling = coupling.reshape(sup_section * block_size, sup_local * block_size)
    mine, other = coupling[:rows], coupling[rows:]
    width = width_cols // CHUNKS
    fronts = [(front_in[:, c * width : (c + 1) * width],) for c in range(CHUNKS)]
    sections = lax.axis_size("chain")
    direct = [(s * halves + i, (s + 1) * halves + i) for s in range(sections - 1) for i in range(halves)]
    crossed = [
        (s * halves + i, (s + 2) * halves - 1 - i) for s in range(sections - 1) for i in range(halves)
    ]
    axes = ("chain", "col")
    earlier = None
    solved_rows = []
    for tick_index in range(tick_count):
        solved_chunks = []
        for c in range(CHUNKS):
            parts = fronts[c]
            values = rhs[tick_index, :, c * width : (c + 1) * width]
            if earlier is not None:
                parts, values, _ = lax.optimization_barrier((parts, values, earlier))
            for part in parts:
                values = values - part
            shaped = values.reshape(sup_local, block_size, width)
            solved = jnp.einsum("nij,njw->niw", diag_inverse, shaped, precision=HIGH)
            flat = solved.reshape(rows, width)
            solved_chunks.append(flat)
            send = jnp.dot(other, flat, precision=HIGH)
            again, _ = lax.optimization_barrier((flat, send))
            kept = jnp.dot(mine, again, precision=HIGH)
            fronts[c] = (lax.ppermute(send, axes, crossed), lax.ppermute(kept, axes, direct))
            earlier = kept
        solved_rows.append(jnp.concatenate(solved_chunks, axis=1))
    return (jnp.stack(solved_rows), jnp.concatenate([a + b for a, b in fronts], axis=1))


def solution(mesh):
    return jax.shard_map(
        local,
        mesh=mesh,
        in_specs=(
            P(("chain", "col"), None, None),
            P(("chain", "col"), None, None),
            P(("chain", "col")),
            P(("chain", "col")),
            P(None, ("chain", "col"), None),
            P(("chain", "col"), None),
        ),
        out_specs=(P(None, ("chain", "col"), None), P(("chain", "col"), None)),
        check_vma=False,
    )
```

```python
import functools

import jax
import jax.numpy as jnp
from jax import lax
from jax.experimental import pallas as pl
from jax.experimental.pallas import tpu as pltpu
from jax.sharding import PartitionSpec as P

CHUNKS = 2
VMEM_LIMIT = 24 * 1024 * 1024


def split(value):
    high = value.astype(jnp.bfloat16)
    return high, (value - high.astype(jnp.float32)).astype(jnp.bfloat16)


def wide(value):
    high, low = split(value)
    return jnp.concatenate([high, high, low], axis=1)


def tall(value):
    high, low = split(value)
    return jnp.concatenate([high, low, high], axis=0)


def product(left, right):
    return jnp.dot(left, right, preferred_element_type=jnp.float32)


def solve_and_couple(row_ref, col_ref, diag, blocks, values_of, solved_ref, send_ref, keep_ref, tall_ref, sum_ref):
    sups, order = tall_ref.shape[0], solved_ref.shape[0] // tall_ref.shape[0]
    section = sum_ref.shape[0]
    start = lax.axis_index("col") * sups
    for n in range(sups):
        solved = product(diag(n), tall(values_of(pl.ds(n * order, order))))
        solved_ref[pl.ds(n * order, order), :] = solved
        tall_ref[n] = tall(solved)
    sum_ref[...] = jnp.zeros_like(sum_ref)
    for k in range(row_ref.shape[0]):
        row = row_ref[k] - start
        row = jnp.where(row < 0, row + section, row)
        sum_ref[row] += product(blocks(k), tall_ref[col_ref[k] - start])
    for n in range(sups):
        keep_ref[pl.ds(n * order, order), :] = sum_ref[n]
        send_ref[pl.ds(n * order, order), :] = sum_ref[sups + n]


def first_kernel(row_ref, col_ref, diag_ref, block_ref, rhs_ref, front_ref, solved_ref, send_ref, keep_ref, dwide_ref, bwide_ref, tall_ref, sum_ref):
    for n in range(diag_ref.shape[0]):
        dwide_ref[n] = wide(diag_ref[n])
    for k in range(block_ref.shape[0]):
        bwide_ref[k] = wide(block_ref[k])
    solve_and_couple(
        row_ref, col_ref, lambda n: dwide_ref[n], lambda k: bwide_ref[k],
        lambda at: rhs_ref[0, at, :] - front_ref[at, :],
        solved_ref, send_ref, keep_ref, tall_ref, sum_ref,
    )


def tick_kernel(parts, row_ref, col_ref, dwide_ref, bwide_ref, rhs_ref, *refs):
    fronts, (solved_ref, send_ref, keep_ref, tall_ref, sum_ref) = refs[:parts], refs[parts:]

    def values_of(at):
        value = rhs_ref[at, :]
        for front_ref in fronts:
            value = value - front_ref[at, :]
        return value

    solve_and_couple(
        row_ref, col_ref, lambda n: dwide_ref[n], lambda k: bwide_ref[k], values_of,
        solved_ref, send_ref, keep_ref, tall_ref, sum_ref,
    )


def local(diag_inverse, off_blocks, off_row, off_col, rhs, front_in):
    sup_local, block_size, _ = diag_inverse.shape
    tick_count, rows, width_cols = rhs.shape
    block_count = off_blocks.shape[0]
    halves = lax.axis_size("col")
    sections = lax.axis_size("chain")
    width = width_cols // CHUNKS
    axes = ("chain", "col")
    direct = [(s * halves + i, (s + 1) * halves + i) for s in range(sections - 1) for i in range(halves)]
    crossed = [
        (s * halves + i, (s + 2) * halves - 1 - i) for s in range(sections - 1) for i in range(halves)
    ]
    smem = pl.BlockSpec(memory_space=pltpu.SMEM)
    vmem = pl.BlockSpec(memory_space=pltpu.VMEM)
    piece = jax.ShapeDtypeStruct((rows, width), jnp.float32)
    scratch = [
        pltpu.VMEM((sup_local, 3 * block_size, width), jnp.bfloat16),
        pltpu.VMEM((sup_local * halves, block_size, width), jnp.float32),
    ]
    params = pltpu.CompilerParams(vmem_limit_bytes=VMEM_LIMIT)
    cost = pl.CostEstimate(
        flops=6 * (sup_local + block_count) * block_size * block_size * width,
        bytes_accessed=8 * rows * width * 4, transcendentals=0,
    )
    first = pl.pallas_call(
        first_kernel,
        grid=(1,),
        out_shape=(
            piece, piece, piece,
            jax.ShapeDtypeStruct((sup_local, block_size, 3 * block_size), jnp.bfloat16),
            jax.ShapeDtypeStruct((block_count, block_size, 3 * block_size), jnp.bfloat16),
        ),
        in_specs=[
            smem, smem, vmem, vmem,
            pl.BlockSpec((1, rows, width), lambda i: (0, 0, 0)),
            pl.BlockSpec((rows, width), lambda i: (0, 0)),
        ],
        out_specs=(vmem,) * 5,
        scratch_shapes=scratch,
        compiler_params=params, cost_estimate=cost, name="first",
    )

    def tick(*args):
        return pl.pallas_call(
            functools.partial(tick_kernel, len(args) - 5),
            out_shape=(piece, piece, piece),
            in_specs=[smem, smem] + [vmem] * (len(args) - 2),
            out_specs=(vmem,) * 3,
            scratch_shapes=scratch,
            compiler_params=params, cost_estimate=cost, name="tick",
        )(*args)

    fronts = [(front_in[:, c * width : (c + 1) * width],) for c in range(CHUNKS)]
    solved_rows = []
    earlier = dwide = bwide = None
    for tick_index in range(tick_count):
        solved_chunks = []
        for c in range(CHUNKS):
            if earlier is None:
                solved, send, keep, dwide, bwide = first(off_row, off_col, diag_inverse, off_blocks, rhs, front_in)
            else:
                values = rhs[tick_index, :, c * width : (c + 1) * width]
                parts, values, _ = lax.optimization_barrier((fronts[c], values, earlier))
                solved, send, keep = tick(off_row, off_col, dwide, bwide, values, *parts)
            solved_chunks.append(solved)
            fronts[c] = (lax.ppermute(send, axes, crossed), lax.ppermute(keep, axes, direct))
            earlier = keep
        solved_rows.append(jnp.concatenate(solved_chunks, axis=1))
    return (jnp.stack(solved_rows), jnp.concatenate([a + b for a, b in fronts], axis=1))


def solution(mesh):
    return jax.shard_map(
        local,
        mesh=mesh,
        in_specs=(
            P(("chain", "col"), None, None),
            P(("chain", "col"), None, None),
            P(("chain", "col")),
            P(("chain", "col")),
            P(None, ("chain", "col"), None),
            P(("chain", "col"), None),
        ),
        out_specs=(P(None, ("chain", "col"), None), P(("chain", "col"), None)),
        check_vma=False,
    )
```

```python
import functools

import jax
import jax.numpy as jnp
from jax import lax
from jax.experimental import pallas as pl
from jax.experimental.pallas import tpu as pltpu
from jax.sharding import PartitionSpec as P

CHUNKS = 2
VMEM_LIMIT = 24 * 1024 * 1024


def split(value):
    high = value.astype(jnp.bfloat16)
    return high, (value - high.astype(jnp.float32)).astype(jnp.bfloat16)


def wide(value):
    high, low = split(value)
    return jnp.concatenate([high, high, low], axis=1)


def product(left, right):
    depth = right.shape[0] // 2
    return jnp.dot(left[:, : 2 * depth], right, preferred_element_type=jnp.float32) + jnp.dot(
        left[:, 2 * depth :], right[:depth], preferred_element_type=jnp.float32
    )


def solve_and_couple(row_ref, col_ref, indices, diag, blocks, values_of, solved_ref, send_ref, keep_ref, tall_ref, sum_ref):
    sups, order = tall_ref.shape[0], solved_ref.shape[0] // tall_ref.shape[0]
    section = sum_ref.shape[0]
    start = lax.axis_index("col") * sups
    for n in range(sups):
        values = jnp.concatenate(split(values_of(pl.ds(n * order, order))), axis=0)
        solved = product(diag(n), values)
        solved_ref[pl.ds(n * order, order), :] = solved
        tall_ref[n] = jnp.concatenate(split(solved), axis=0)
    sum_ref[...] = jnp.zeros_like(sum_ref)
    for copy in indices:
        copy.wait()
    for k in range(row_ref.shape[0]):
        row = row_ref[k] - start
        row = jnp.where(row < 0, row + section, row)
        sum_ref[row] += product(blocks(k), tall_ref[col_ref[k] - start])
    for n in range(sups):
        send_ref[pl.ds(n * order, order), :] = sum_ref[sups + n]
        keep_ref[pl.ds(n * order, order), :] = sum_ref[n]


def index_copies(row_hbm, col_hbm, row_ref, col_ref, sems):
    copies = (
        pltpu.make_async_copy(row_hbm, row_ref, sems.at[0]),
        pltpu.make_async_copy(col_hbm, col_ref, sems.at[1]),
    )
    for copy in copies:
        copy.start()
    return copies


def first_kernel(
    row_hbm, col_hbm, diag_hbm, block_hbm, rhs_hbm, front_hbm, solved_ref, send_ref, keep_ref, dwide_ref, bwide_ref,
    tall_ref, sum_ref, row_ref, col_ref, index_sems, diag_ref, block_ref, rhs_ref, front_ref, sems,
):
    width = rhs_ref.shape[1]
    copies = (
        pltpu.make_async_copy(diag_hbm, diag_ref, sems.at[0]),
        pltpu.make_async_copy(front_hbm.at[:, pl.ds(0, width)], front_ref, sems.at[1]),
        pltpu.make_async_copy(rhs_hbm.at[0, :, pl.ds(0, width)], rhs_ref, sems.at[2]),
        pltpu.make_async_copy(block_hbm, block_ref, sems.at[3]),
    )
    for copy in copies:
        copy.start()
    indices = index_copies(row_hbm, col_hbm, row_ref, col_ref, index_sems)
    copies[0].wait()
    for n in range(diag_ref.shape[0]):
        dwide_ref[n] = wide(diag_ref[n])
    for copy in copies[1:]:
        copy.wait()
    for k in range(block_ref.shape[0]):
        bwide_ref[k] = wide(block_ref[k])
    solve_and_couple(
        row_ref, col_ref, indices, lambda n: dwide_ref[n], lambda k: bwide_ref[k],
        lambda at: rhs_ref[at, :] - front_ref[at, :],
        solved_ref, send_ref, keep_ref, tall_ref, sum_ref,
    )


def tick_kernel(parts, row_hbm, col_hbm, dwide_ref, bwide_ref, rhs_ref, *refs):
    fronts, (solved_ref, send_ref, keep_ref, tall_ref, sum_ref, row_ref, col_ref, index_sems) = refs[:parts], refs[parts:]
    indices = index_copies(row_hbm, col_hbm, row_ref, col_ref, index_sems)

    def values_of(at):
        value = rhs_ref[at, :]
        for front_ref in fronts:
            value = value - front_ref[at, :]
        return value

    solve_and_couple(
        row_ref, col_ref, indices, lambda n: dwide_ref[n], lambda k: bwide_ref[k], values_of,
        solved_ref, send_ref, keep_ref, tall_ref, sum_ref,
    )


def local(diag_inverse, off_blocks, off_row, off_col, rhs, front_in):
    sup_local, block_size, _ = diag_inverse.shape
    tick_count, rows, width_cols = rhs.shape
    block_count = off_blocks.shape[0]
    halves = lax.axis_size("col")
    sections = lax.axis_size("chain")
    width = width_cols // CHUNKS
    axes = ("chain", "col")
    direct = [(s * halves + i, (s + 1) * halves + i) for s in range(sections - 1) for i in range(halves)]
    crossed = [
        (s * halves + i, (s + 2) * halves - 1 - i) for s in range(sections - 1) for i in range(halves)
    ]
    hbm = pl.BlockSpec(memory_space=pltpu.HBM)
    vmem = pl.BlockSpec(memory_space=pltpu.VMEM)
    piece = jax.ShapeDtypeStruct((rows, width), jnp.float32)
    scratch = [
        pltpu.VMEM((sup_local, 2 * block_size, width), jnp.bfloat16),
        pltpu.VMEM((sup_local * halves, block_size, width), jnp.float32),
        pltpu.SMEM((block_count,), jnp.int32),
        pltpu.SMEM((block_count,), jnp.int32),
        pltpu.SemaphoreType.DMA((2,)),
    ]
    params = pltpu.CompilerParams(vmem_limit_bytes=VMEM_LIMIT)
    cost = pl.CostEstimate(
        flops=6 * (sup_local + block_count) * block_size * block_size * width,
        bytes_accessed=8 * rows * width * 4, transcendentals=0,
    )
    first = pl.pallas_call(
        first_kernel,
        out_shape=(
            piece, piece, piece,
            jax.ShapeDtypeStruct((sup_local, block_size, 3 * block_size), jnp.bfloat16),
            jax.ShapeDtypeStruct((block_count, block_size, 3 * block_size), jnp.bfloat16),
        ),
        in_specs=[hbm] * 6,
        out_specs=(vmem,) * 5,
        scratch_shapes=scratch + [
            pltpu.VMEM((sup_local, block_size, block_size), jnp.float32),
            pltpu.VMEM((block_count, block_size, block_size), jnp.float32),
            pltpu.VMEM((rows, width), jnp.float32),
            pltpu.VMEM((rows, width), jnp.float32),
            pltpu.SemaphoreType.DMA((4,)),
        ],
        compiler_params=params, cost_estimate=cost, name="first",
    )

    def tick(*args):
        return pl.pallas_call(
            functools.partial(tick_kernel, len(args) - 5),
            out_shape=(piece, piece, piece),
            in_specs=[hbm, hbm] + [vmem] * (len(args) - 2),
            out_specs=(vmem,) * 3,
            scratch_shapes=scratch,
            compiler_params=params, cost_estimate=cost, name="tick",
        )(*args)

    solved_rows = []
    earlier = dwide = bwide = None
    for tick_index in range(tick_count):
        solved_chunks = []
        for c in range(CHUNKS):
            if earlier is None:
                solved, send, keep, dwide, bwide = first(*(pltpu.with_memory_space_constraint(a, pltpu.HBM) for a in (off_row, off_col, diag_inverse, off_blocks, rhs, front_in)))
                later_rhs, later_front, _ = lax.optimization_barrier((rhs, front_in, keep))
                fronts = [(later_front[:, i * width : (i + 1) * width],) for i in range(CHUNKS)]
            else:
                values = later_rhs[tick_index, :, c * width : (c + 1) * width]
                parts, values, _ = lax.optimization_barrier((fronts[c], values, earlier))
                solved, send, keep = tick(off_row, off_col, dwide, bwide, values, *parts)
            solved_chunks.append(solved)
            fronts[c] = (lax.ppermute(send, axes, crossed), lax.ppermute(keep, axes, direct))
            earlier = keep
        solved_rows.append(jnp.concatenate(solved_chunks, axis=1))
    return (jnp.stack(solved_rows), jnp.concatenate([a + b for a, b in fronts], axis=1))


def solution(mesh):
    return jax.shard_map(
        local,
        mesh=mesh,
        in_specs=(
            P(("chain", "col"), None, None),
            P(("chain", "col"), None, None),
            P(("chain", "col")),
            P(("chain", "col")),
            P(None, ("chain", "col"), None),
            P(("chain", "col"), None),
        ),
        out_specs=(P(None, ("chain", "col"), None), P(("chain", "col"), None)),
        check_vma=False,
    )
```

```python
import functools

import jax
import jax.numpy as jnp
from jax import lax
from jax.experimental import pallas as pl
from jax.experimental.pallas import tpu as pltpu
from jax.sharding import PartitionSpec as P

VMEM_LIMIT = 20 * 1024 * 1024
CHUNKS = 3
SUBLANES = 16


def chunks_of(width):
    tiles = width // SUBLANES
    sizes = [(tiles // CHUNKS + (c < tiles % CHUNKS)) * SUBLANES for c in range(CHUNKS)]
    return [(sum(sizes[:c]), sizes[c]) for c in range(CHUNKS)]


def split(value):
    high = value.astype(jnp.bfloat16)
    return high, (value - high.astype(jnp.float32)).astype(jnp.bfloat16)


def matrix_form(value):
    high, low = split(value)
    return jnp.concatenate([high, high, low], axis=1)


def vector_form(value):
    return jnp.concatenate(split(value), axis=1)


def times(vectors, matrix):
    depth = vectors.shape[1] // 2
    contract = (((1,), (1,)), ((), ()))
    return lax.dot_general(
        vectors, matrix[:, : 2 * depth], contract, preferred_element_type=jnp.float32
    ) + lax.dot_general(
        vectors[:, :depth], matrix[:, 2 * depth :], contract, preferred_element_type=jnp.float32
    )


def index_copies(row_hbm, col_hbm, row_ref, col_ref, sems):
    copies = (
        pltpu.make_async_copy(row_hbm, row_ref, sems.at[0]),
        pltpu.make_async_copy(col_hbm, col_ref, sems.at[1]),
    )
    for copy in copies:
        copy.start()
    return copies


def solve_and_couple(indices, dform_ref, bform_ref, values_of, solved_ref, send_ref, keep_ref, xform_ref, sum_ref, row_ref, col_ref):
    sups, section = xform_ref.shape[0], sum_ref.shape[0]
    start = lax.axis_index("col") * sups
    for n in range(sups):
        solved = times(vector_form(values_of(n)), dform_ref[n])
        solved_ref[n] = solved
        xform_ref[n] = vector_form(solved)
    sum_ref[...] = jnp.zeros_like(sum_ref)
    for copy in indices:
        copy.wait()
    for k in range(bform_ref.shape[0]):
        row = row_ref[k] - start
        row = jnp.where(row < 0, row + section, row)
        sum_ref[row] += times(xform_ref[col_ref[k] - start], bform_ref[k])
    send_ref[...] = sum_ref[sups:]
    keep_ref[...] = sum_ref[:sups]


def first_kernel(
    row_hbm, col_hbm, diag_hbm, block_hbm, rhs_hbm, front_hbm, solved_ref, send_ref, keep_ref, dform_ref, bform_ref,
    xform_ref, sum_ref, row_ref, col_ref, index_sems, diag_ref, block_ref, rhs_ref, front_ref, sems,
):
    lanes = rhs_ref.shape[1]
    sups, order, _ = diag_ref.shape
    width = solved_ref.shape[1]
    copies = (
        pltpu.make_async_copy(diag_hbm, diag_ref, sems.at[0]),
        pltpu.make_async_copy(front_hbm.at[:, pl.ds(0, lanes)], front_ref, sems.at[1]),
        pltpu.make_async_copy(rhs_hbm.at[0, :, pl.ds(0, lanes)], rhs_ref, sems.at[2]),
        pltpu.make_async_copy(block_hbm, block_ref, sems.at[3]),
    )
    for copy in copies:
        copy.start()
    indices = index_copies(row_hbm, col_hbm, row_ref, col_ref, index_sems)
    copies[0].wait()
    for n in range(sups):
        dform_ref[n] = matrix_form(diag_ref[n])
    for copy in copies[1:]:
        copy.wait()
    for k in range(block_ref.shape[0]):
        bform_ref[k] = matrix_form(block_ref[k])

    def values_of(n):
        at = pl.ds(n * order, order)
        return (rhs_ref[at, :] - front_ref[at, :]).T[:width]

    solve_and_couple(
        indices, dform_ref, bform_ref, values_of, solved_ref, send_ref, keep_ref, xform_ref, sum_ref, row_ref, col_ref
    )


def tick_kernel(parts, offset, row_hbm, col_hbm, dform_ref, bform_ref, rhs_ref, *refs):
    fronts, rest = refs[:parts], refs[parts:]
    solved_ref, send_ref, keep_ref, xform_ref, sum_ref, row_ref, col_ref, index_sems = rest
    indices = index_copies(row_hbm, col_hbm, row_ref, col_ref, index_sems)
    width = solved_ref.shape[1]

    def values_of(n):
        value = rhs_ref[n, pl.ds(offset, width), :]
        for front_ref in fronts:
            value = value - front_ref[n]
        return value

    solve_and_couple(
        indices, dform_ref, bform_ref, values_of, solved_ref, send_ref, keep_ref, xform_ref, sum_ref, row_ref, col_ref
    )


def turn_kernel(tick_index, rhs_ref, *refs):
    *front, out_ref = refs
    sups, _, order = out_ref.shape
    for n in range(sups):
        at = pl.ds(n * order, order)
        value = rhs_ref[tick_index, at, :]
        for front_ref in front:
            value = value - front_ref[at, :]
        out_ref[n] = value.T


def back_kernel(counts, tick_index, *refs):
    terms = CHUNKS * counts
    chunks, out_hbm, tile_ref, sems = refs[:terms], refs[-3], refs[-2], refs[-1]
    sups, _, order = chunks[0].shape
    target = out_hbm if tick_index is None else out_hbm.at[tick_index]
    copies = []
    for n in range(sups):
        pieces = []
        for c in range(CHUNKS):
            piece = chunks[c * counts][n]
            for i in range(1, counts):
                piece = piece + chunks[c * counts + i][n]
            pieces.append(piece)
        at = pl.ds(n * order, order)
        tile_ref[at, :] = jnp.concatenate(pieces, axis=0).T
        copies.append(pltpu.make_async_copy(tile_ref.at[at, :], target.at[at, :], sems.at[n]))
        copies[-1].start()
    for copy in copies:
        copy.wait()


def local(diag_inverse, off_blocks, off_row, off_col, rhs, front_in):
    sup_local, block_size, _ = diag_inverse.shape
    tick_count, rows, width_cols = rhs.shape
    block_count = off_blocks.shape[0]
    halves = lax.axis_size("col")
    sections = lax.axis_size("chain")
    chunks = chunks_of(width_cols)
    axes = ("chain", "col")
    direct = [(s * halves + i, (s + 1) * halves + i) for s in range(sections - 1) for i in range(halves)]
    crossed = [
        (s * halves + i, (s + 2) * halves - 1 - i) for s in range(sections - 1) for i in range(halves)
    ]
    hbm = pl.BlockSpec(memory_space=pltpu.HBM)
    vmem = pl.BlockSpec(memory_space=pltpu.VMEM)
    params = pltpu.CompilerParams(vmem_limit_bytes=VMEM_LIMIT)
    f32, bf16 = jnp.float32, jnp.bfloat16

    def in_hbm(*arrays):
        return [pltpu.with_memory_space_constraint(a, pltpu.HBM) for a in arrays]

    def shared(width):
        piece = jax.ShapeDtypeStruct((sup_local, width, block_size), f32)
        scratch = [
            pltpu.VMEM((sup_local, width, 2 * block_size), bf16),
            pltpu.VMEM((sup_local * halves, width, block_size), f32),
            pltpu.SMEM((block_count,), jnp.int32),
            pltpu.SMEM((block_count,), jnp.int32),
            pltpu.SemaphoreType.DMA((2,)),
        ]
        cost = pl.CostEstimate(
            flops=6 * (sup_local + block_count) * block_size * block_size * width,
            bytes_accessed=8 * rows * width * 4, transcendentals=0,
        )
        return piece, scratch, cost

    def first():
        piece, scratch, cost = shared(chunks[0][1])
        return pl.pallas_call(
            first_kernel,
            out_shape=(
                piece, piece, piece,
                jax.ShapeDtypeStruct((sup_local, block_size, 3 * block_size), bf16),
                jax.ShapeDtypeStruct((block_count, block_size, 3 * block_size), bf16),
            ),
            in_specs=[hbm] * 6,
            out_specs=(vmem,) * 5,
            scratch_shapes=scratch + [
                pltpu.VMEM((sup_local, block_size, block_size), f32),
                pltpu.VMEM((block_count, block_size, block_size), f32),
                pltpu.VMEM((rows, block_size), f32),
                pltpu.VMEM((rows, block_size), f32),
                pltpu.SemaphoreType.DMA((4,)),
            ],
            compiler_params=params, cost_estimate=cost, name="first",
        )(*in_hbm(off_row, off_col, diag_inverse, off_blocks, rhs, front_in))

    def tick(chunk, *args):
        offset, width = chunks[chunk]
        piece, scratch, cost = shared(width)
        return pl.pallas_call(
            functools.partial(tick_kernel, len(args) - 5, offset),
            out_shape=(piece, piece, piece),
            in_specs=[hbm, hbm] + [vmem] * (len(args) - 2),
            out_specs=(vmem,) * 3,
            scratch_shapes=scratch,
            compiler_params=params, cost_estimate=cost, name=f"tick{chunk}",
        )(*args)

    moves = pl.CostEstimate(flops=0, bytes_accessed=2 * rows * width_cols * 4, transcendentals=0)

    def turn(tick_index, *args):
        return pl.pallas_call(
            functools.partial(turn_kernel, tick_index),
            out_shape=jax.ShapeDtypeStruct((sup_local, width_cols, block_size), f32),
            in_specs=[vmem] * len(args),
            out_specs=vmem,
            compiler_params=params, cost_estimate=moves, name="turn",
        )(*args)

    def back(pieces, tick_index=None, into=None):
        terms = [term for piece in pieces for term in piece]
        shape = (rows, width_cols) if tick_index is None else (tick_count, rows, width_cols)
        more = [] if into is None else [into]
        return pl.pallas_call(
            functools.partial(back_kernel, len(pieces[0]), tick_index),
            out_shape=pltpu.HBM(shape, f32),
            in_specs=[vmem] * len(terms) + [hbm] * len(more),
            out_specs=hbm,
            scratch_shapes=[pltpu.VMEM((rows, width_cols), f32), pltpu.SemaphoreType.DMA((sup_local,))],
            input_output_aliases={len(terms): 0} if more else {},
            compiler_params=params, cost_estimate=moves, name="back",
        )(*terms, *more)

    fronts = [()] * CHUNKS
    solutions = dform = bform = None
    previous = None
    for tick_index in range(tick_count):
        solved_chunks = []
        for c in range(CHUNKS):
            if tick_index == 0 and c == 0:
                solved, send, keep, dform, bform = first()
                later_rhs, later_front, _ = lax.optimization_barrier((rhs, front_in, keep))
                turned = turn(0, later_rhs, later_front)
            else:
                parts, values, _ = lax.optimization_barrier((fronts[c], turned, keep))
                solved, send, keep = tick(c, off_row, off_col, dform, bform, values, *parts)
            solved_chunks.append((solved,))
            fronts[c] = (lax.ppermute(send, axes, crossed), lax.ppermute(keep, axes, direct))
            if c == 1 and tick_index + 1 < tick_count:
                this_rhs, keep = lax.optimization_barrier((later_rhs, keep))
                next_turned = turn(tick_index + 1, this_rhs)
            if c == 0 and previous is not None:
                done, keep = lax.optimization_barrier((previous, keep))
                solutions = back(done, tick_index - 1, solutions)
        turned = next_turned
        previous = solved_chunks
    solutions = back(previous, tick_count - 1, solutions)
    sums = []
    for parts in fronts:
        if sums:
            parts, sums[-1] = lax.optimization_barrier((parts, sums[-1]))
        sums.append(parts[0] + parts[1])
    return (solutions, back([(total,) for total in sums]))


def solution(mesh):
    return jax.shard_map(
        local,
        mesh=mesh,
        in_specs=(
            P(("chain", "col"), None, None),
            P(("chain", "col"), None, None),
            P(("chain", "col")),
            P(("chain", "col")),
            P(None, ("chain", "col"), None),
            P(("chain", "col"), None),
        ),
        out_specs=(P(None, ("chain", "col"), None), P(("chain", "col"), None)),
        check_vma=False,
    )
```
